32 devices in a mesh: parts: 2 (over x), blk: 16 (over z, y, core).
Axes of the slice: x: 2, y: 2, z: 4, core: 2. Of those that a mesh axis runs over, the one named last changes fastest.
Arguments:
- activations: bfloat16 [32, 160, 4096], P(('parts', 'blk')), parts along dimension 0, may hold values from -6 to 6
- output_grads: bfloat16 [32, 160, 14336], P(('parts', 'blk')), parts along dimension 0, may hold values from -6 to 6
- basis_in: bfloat16 [4096, 4096], P('blk'), may hold values from -0.09375 to 0.09375
- basis_out: bfloat16 [14336, 14336], P('blk'), may hold values from -0.046875 to 0.046875
- query_left: bfloat16 [16, 32, 4096], P('blk'), may hold values from -0.09375 to 0.09375
- query_right: bfloat16 [16, 32, 14336], P('blk'), may hold values from -0.046875 to 0.046875
- owners: int32 [4], replicated, may hold values from 0 to 15, as said below
- lengths: int32 [32], P('parts'), parts along dimension 0, may hold values from 1 to 160, 1920 in all
- slot_plan: int32 [32], P('parts'), parts along dimension 0, may hold values from 0 to 15, each once
Outputs:
- scores: float32 [32, 4], P(('parts', 'blk')), parts along dimension 0
The draws below stay inside these ranges and needn't reach their ends.
There are 2 independent parts, one for each index of `parts`. The reference program is written for one: setup_inputs(seed, part) draws one part's arguments, and reference() takes and returns one part's arrays. A program takes and returns all parts, laid end to end along the dimension named above; an argument that names none is the same for every part. Nothing has to cross between parts.
Inputs may be any that keep to these rules, and one draw needn't show every extreme that they name: `owners`: distinct slots of blk.
All inputs are finite; a program needn't handle non-finite values.
Results may differ from the reference program's by a relative error of at most 0.01.
Values may be sent and summed in bfloat16 or wider, within the bound.
A program may use at most 128 MiB of HBM per device.

```python
import math
import jax
import jax.numpy as jnp
import numpy as np
from jax import lax

D = 4096
FF = 14336
FW = 14336
R = 32
QUERIES = 4
LMAX = 160
SEQS = 16
TOKENS = 2560
N_BLK = 16


def draw_owners(key, part):
    return jax.random.permutation(key, N_BLK)[:QUERIES].astype(jnp.int32)


def block_scale(rng, dims, cuts, low, high):
    def one(dim, parts):
        draws = jax.random.uniform(jax.random.fold_in(jax.random.fold_in(rng, 6), dim), (parts,), jnp.float32, low / len(cuts), high / len(cuts))
        return jnp.repeat(jnp.exp(draws), dims[dim] // parts).reshape((-1,) + (1,) * (len(dims) - dim - 1))

    level = one(*cuts[0])
    for cut in cuts[1:]:
        level = level * one(*cut)
    return level


def profile(count, total, bound, skew):
    loads = [(1 << 20) // math.isqrt(rank ** skew) + 1 for rank in range(2, count + 1)]
    rest, holding = total - bound - (count - 1), [1] * (count - 1)
    while rest > 0:
        free = [i for i in range(count - 1) if holding[i] < bound]
        mass, left = sum([loads[i] for i in free]), rest
        for i in free:
            addition = min(bound - holding[i], max(1, left * loads[i] // mass), rest)
            holding[i] = holding[i] + addition
            rest = rest - addition
    return np.array([bound] + holding)


def ragged_sizes(own_key, number_of, total, limit, slope):
    if number_of == 2:
        one = jax.random.randint(own_key, (), max(1, total - limit), min(limit, total - 1) + 1)
        return jnp.stack([one, total - one])
    sizes = jnp.asarray(profile(number_of, total, limit, slope), jnp.int32)
    twos = (number_of - 1) // 2
    giver, sink = sizes[1:1 + 2 * twos:2], sizes[2:2 + 2 * twos:2]
    room = jnp.minimum(giver - 1, limit - sink)
    passed = jax.random.randint(jax.random.fold_in(own_key, 1), (twos,), 0, 1 << 20) % (room + 1)
    sizes = sizes.at[1:1 + 2 * twos:2].set(giver - passed).at[2:2 + 2 * twos:2].set(sink + passed)
    return sizes[jax.random.permutation(jax.random.fold_in(own_key, 2), number_of)]


def centred(stream_key, shape, spread, bound, shards=(), kind=jnp.bfloat16):
    factor_of = block_scale(stream_key, shape, shards, -0.22, 0.18) if shards else 1.0
    values = jax.random.normal(stream_key, shape, jnp.float32) * spread * factor_of
    return jnp.minimum(jnp.maximum(values, -bound), bound).astype(kind)


def setup_inputs(seed: int = 0, part: int = 0) -> dict:
    splits = jax.random.split(jax.random.key(seed), 10)
    part_keys = jax.random.split(jax.random.fold_in(splits[9], part), 10)
    return {
        "activations": centred(part_keys[0], (SEQS, LMAX, D), 1.0, 6.0, ((0, 16),)),
        "output_grads": centred(part_keys[1], (SEQS, LMAX, FF), 1.0, 6.0, ((0, 16),)),
        "basis_in": centred(splits[2], (D, D), D ** -0.5, 0.09375, ((0, 16),)),
        "basis_out": centred(splits[3], (FF, FW), FF ** -0.5, 0.046875, ((0, 16),)),
        "query_left": centred(splits[4], (N_BLK, R, D), D ** -0.5, 0.09375, ((0, 16),)),
        "query_right": centred(splits[5], (N_BLK, R, FW), FW ** -0.5, 0.046875, ((0, 16),)),
        "owners": draw_owners(jax.random.fold_in(splits[9], 71), part),
        "lengths": ragged_sizes(part_keys[7], SEQS, SEQS * LMAX * 3 // 4, LMAX, 2).astype(jnp.int32),
        "slot_plan": jax.random.permutation(part_keys[8], SEQS).astype(jnp.int32),
    }


def reference(activations, output_grads, basis_in, basis_out, query_left, query_right, owners, lengths, slot_plan):
    left = query_left[owners].reshape(QUERIES * R, D)
    right = query_right[owners].reshape(QUERIES * R, FW)
    contract = (((1,), (1,)), ((), ()))
    rotated_in = lax.dot_general(basis_in, left, contract, preferred_element_type=jnp.float32).astype(jnp.bfloat16)
    rotated_out = lax.dot_general(basis_out, right, contract, preferred_element_type=jnp.float32).astype(jnp.bfloat16)
    project_in = jnp.dot(activations.reshape(TOKENS, D), rotated_in, preferred_element_type=jnp.float32)
    project_out = jnp.dot(output_grads.reshape(TOKENS, FF), rotated_out, preferred_element_type=jnp.float32)
    products = (project_in * project_out).reshape(SEQS, LMAX, QUERIES, R)
    slot_lengths = lengths[slot_plan]
    live_mask = (jnp.arange(LMAX)[None, :] < slot_lengths[:, None]).astype(jnp.float32)
    slot_score = jnp.einsum('stqr,st->sq', products, live_mask) / R
    return jnp.zeros((SEQS, QUERIES), jnp.float32).at[slot_plan].set(slot_score)
```

```python
import functools

import jax
import jax.numpy as jnp
from jax import lax
from jax.experimental import pallas as pl
from jax.experimental.pallas import tpu as pltpu
from jax.sharding import PartitionSpec as P

MESH = pl.DeviceIdType.MESH
CORES = 2
LANES = 128


def ring_order(chips):
    cols = 1
    while (2 * cols) * (2 * cols) <= chips:
        cols *= 2
    rows = chips // cols
    tour = [r * cols for r in range(rows)]
    for step, r in enumerate(reversed(range(rows))):
        across = range(1, cols) if step % 2 == 0 else range(cols - 1, 0, -1)
        tour += [r * cols + c for c in across]
    return tour


def lookup(index, table):
    found = jnp.int32(0)
    for key, value in enumerate(table):
        found = found + jnp.where(index == key, jnp.int32(value), jnp.int32(0))
    return found


def fused_kernel(
    n,
    act_hbm,
    grad_hbm,
    bin_hbm,
    bout_hbm,
    ql_hbm,
    qr_hbm,
    owners,
    lengths,
    slot_plan,
    out_ref,
    act,
    grad,
    bin_,
    bout,
    slots,
    gathered,
    rotated,
    acc_in,
    acc_out,
    proj_in,
    proj_out,
    tiles,
    load_sem,
    own_sem,
    a2a_send,
    a2a_recv,
    x_send,
    x_recv,
    ring_send,
    ring_recv,
    sib_send,
    sib_recv,
    tile_send,
    tile_recv,
):
    part = lax.axis_index("parts")
    me = lax.axis_index("blk")
    chips = n // CORES
    core = lax.rem(me, CORES)
    chip = me // CORES
    tour = ring_order(chips)
    place = lookup(chip, [tour.index(c) for c in range(chips)])
    sibling = chip * CORES + (1 - core)
    d_blk = act.shape[1] // n
    f_blk = grad.shape[1] // n
    both = d_blk + f_blk
    rank = ql_hbm.shape[1]
    half_rank = rank // 2
    queries = owners.shape[0]
    sub_rows = queries * half_rank
    far = chips // 2

    def at_distance(h, way, which_core):
        spot = lax.rem(place - h + chips, chips) if way == 0 else lax.rem(place + h, chips)
        return lookup(spot, tour) * CORES + which_core

    right = at_distance(1, 1, core)
    left = at_distance(1, 0, core)

    loads = []

    def load(src, dst):
        copy = pltpu.make_async_copy(src, dst, load_sem.at[len(loads)])
        copy.start()
        loads.append(copy)

    barrier = pltpu.get_barrier_semaphore()
    for k in range(1, n):
        pl.semaphore_signal(
            barrier, inc=1, device_id={"blk": lax.rem(me + k, n)}, device_id_type=MESH
        )
    pl.semaphore_signal(barrier, inc=1, device_id={"parts": 1 - part}, device_id_type=MESH)

    my_rows = pl.ds(pl.multiple_of(part * half_rank, half_rank), half_rank)

    def cut(target, width):
        return pl.ds(pl.multiple_of(target * width, LANES), width)

    own = [
        pltpu.make_async_copy(
            ql_hbm.at[0, my_rows, cut(me, d_blk)], slots.at[me, :, pl.ds(0, d_blk)], own_sem.at[0]
        ),
        pltpu.make_async_copy(
            qr_hbm.at[0, my_rows, cut(me, f_blk)],
            slots.at[me, :, pl.ds(d_blk, f_blk)],
            own_sem.at[1],
        ),
    ]
    for copy in own:
        copy.start()
    pl.semaphore_wait(barrier, n)

    swaps = []
    for k in range(1, n):
        target = lax.rem(me + k, n)
        for piece, (src, width, start) in enumerate(((ql_hbm, d_blk, 0), (qr_hbm, f_blk, d_blk))):
            copy = pltpu.make_async_remote_copy(
                src_ref=src.at[0, my_rows, cut(target, width)],
                dst_ref=slots.at[me, :, pl.ds(start, width)],
                send_sem=a2a_send.at[k, piece],
                recv_sem=a2a_recv.at[k, piece],
                device_id={"blk": target},
                device_id_type=MESH,
            )
            copy.start()
            swaps.append(copy)

    load(bin_hbm, bin_)
    quarter = bout.shape[0] // 4
    for i in range(4):
        span = pl.ds(i * quarter, quarter)
        load(bout_hbm.at[span], bout.at[span])
    load(act_hbm.at[0], act)
    load(grad_hbm.at[0], grad)
    acc_in[...] = jnp.zeros_like(acc_in)
    acc_out[...] = jnp.zeros_like(acc_out)
    proj_in[...] = jnp.zeros_like(proj_in)
    proj_out[...] = jnp.zeros_like(proj_out)

    for copy in own:
        copy.wait()
    for copy in swaps:
        copy.wait_recv()
    first = pl.multiple_of(part * sub_rows, sub_rows)
    for q in range(queries):
        gathered[me, pl.ds(pl.multiple_of(first + q * half_rank, half_rank), half_rank), :] = slots[
            owners[q]
        ]

    def spread(buffer, phase, sub, before_sub, compute):
        limit = ((far, far - 1), (far - 1, far))
        started = []

        def hop(u, way, h):
            block = at_distance(h, way, core)
            view = buffer.at[block, sub(u)]
            copy = pltpu.make_async_remote_copy(
                src_ref=view,
                dst_ref=view,
                send_sem=ring_send.at[phase, u, way, h],
                recv_sem=ring_recv.at[phase, u, way, h],
                device_id={"blk": right if way == 0 else left},
                device_id_type=MESH,
            )
            copy.start()
            started.append(copy)

        def arrival(u, way, h):
            view = buffer.at[at_distance(h, way, core), sub(u)]
            pltpu.make_async_remote_copy(
                src_ref=view,
                dst_ref=view,
                send_sem=ring_send.at[phase, u, way, h - 1],
                recv_sem=ring_recv.at[phase, u, way, h - 1],
                device_id={"blk": right if way == 0 else left},
                device_id_type=MESH,
            ).wait_recv()

        def aside(u, way, h, which_core):
            view = buffer.at[at_distance(h, way, which_core), sub(u)]
            return pltpu.make_async_remote_copy(
                src_ref=view,
                dst_ref=view,
                send_sem=sib_send.at[phase, u, way, h],
                recv_sem=sib_recv.at[phase, u, way, h],
                device_id={"blk": sibling},
                device_id_type=MESH,
            )

        for h in range(far + 1):
            here = []
            for u in range(2):
                if h == 0:
                    before_sub(u)
                ways = [w for w in range(2) if h <= limit[u][w]] if h else [0]
                for way in ways:
                    if h:
                        arrival(u, way, h)
                        if h < limit[u][way]:
                            hop(u, way, h)
                    else:
                        hop(u, 0, 0)
                        hop(u, 1, 0)
                    copy = aside(u, way, h, core)
                    copy.start()
                    started.append(copy)
                    here.append((u, way, h))
            directions = [0] if h in (0, far) else [0, 1]
            compute([at_distance(h, way, core) for way in directions], h == 0)
            for u, way, _ in here:
                aside(u, way, h, 1 - core).wait_recv()
            compute([at_distance(h, way, 1 - core) for way in directions], False)
        return started

    over_last = (((1,), (1,)), ((), ()))

    def each(blocks, body):
        def step(i, carry):
            block = blocks[0]
            for k in range(1, len(blocks)):
                block = jnp.where(i == k, blocks[k], block)
            body(block)
            return carry

        lax.fori_loop(0, len(blocks), step, 0)

    def rotate(block):
        acc_in[...] += lax.dot_general(
            bin_[:, cut(block, d_blk)],
            gathered[block, :, 0:d_blk],
            over_last,
            preferred_element_type=jnp.float32,
        )
        acc_out[...] += lax.dot_general(
            bout[:, cut(block, f_blk)],
            gathered[block, :, d_blk:both],
            over_last,
            preferred_element_type=jnp.float32,
        )

    def rotate_all(blocks, opening):
        if opening:
            for copy in loads:
                copy.wait()
        each(blocks, rotate)

    trade = pltpu.make_async_remote_copy(
        src_ref=gathered.at[me, pl.ds(first, sub_rows)],
        dst_ref=gathered.at[me, pl.ds(first, sub_rows)],
        send_sem=x_send,
        recv_sem=x_recv,
        device_id={"parts": 1 - part},
        device_id_type=MESH,
    )
    trade.start()
    second = pl.multiple_of((1 - part) * sub_rows, sub_rows)

    def before_rotate(u):
        if u == 1:
            pltpu.make_async_remote_copy(
                src_ref=gathered.at[me, pl.ds(second, sub_rows)],
                dst_ref=gathered.at[me, pl.ds(second, sub_rows)],
                send_sem=x_send,
                recv_sem=x_recv,
                device_id={"parts": 1 - part},
                device_id_type=MESH,
            ).wait_recv()

    def sub_query(u):
        return pl.ds(first if u == 0 else second, sub_rows)

    started = spread(gathered, 0, sub_query, before_rotate, rotate_all)

    rotated[me, 0:d_blk, :] = acc_in[...].astype(rotated.dtype)
    rotated[me, d_blk:both, :] = acc_out[...].astype(rotated.dtype)

    def project(block):
        proj_in[...] += jnp.dot(
            act[:, cut(block, d_blk)],
            rotated[block, 0:d_blk, :],
            preferred_element_type=jnp.float32,
        )
        proj_out[...] += jnp.dot(
            grad[:, cut(block, f_blk)],
            rotated[block, d_blk:both, :],
            preferred_element_type=jnp.float32,
        )

    half = both // 2
    started += spread(
        rotated,
        1,
        lambda u: pl.ds(u * half, half),
        lambda u: None,
        lambda blocks, opening: each(blocks, project),
    )

    length = lengths[slot_plan[me]]
    times = lax.broadcasted_iota(jnp.int32, proj_in.shape, 0)
    product = jnp.where(times < length, proj_in[...] * proj_out[...], 0.0)
    by_col = jnp.sum(product, axis=0, keepdims=True)
    col = lax.broadcasted_iota(jnp.int32, by_col.shape, 1)
    col_query = lax.rem(col // half_rank, queries)
    score = jnp.zeros((8, LANES), jnp.float32)
    lane = lax.broadcasted_iota(jnp.int32, score.shape, 1)
    for q in range(queries):
        total = jnp.sum(jnp.where(col_query == q, by_col, 0.0), axis=1, keepdims=True) / rank
        score = jnp.where(lane == q, total, score)
    tiles[me] = score
    pushes = []
    for k in range(1, n):
        copy = pltpu.make_async_remote_copy(
            src_ref=tiles.at[me],
            dst_ref=tiles.at[me],
            send_sem=tile_send.at[k],
            recv_sem=tile_recv.at[k],
            device_id={"blk": lax.rem(me + k, n)},
            device_id_type=MESH,
        )
        copy.start()
        pushes.append(copy)
    for k in range(1, n):
        source = lax.rem(me - k + n, n)
        pltpu.make_async_remote_copy(
            src_ref=tiles.at[source],
            dst_ref=tiles.at[source],
            send_sem=tile_send.at[k],
            recv_sem=tile_recv.at[k],
            device_id={"blk": lax.rem(me + k, n)},
            device_id_type=MESH,
        ).wait_recv()
    mine = jnp.zeros((8, LANES), jnp.float32)
    for j in range(n):
        mine = jnp.where(slot_plan[j] == me, tiles[j], mine)
    out_ref[...] = mine
    for copy in swaps + [trade] + started + pushes:
        copy.wait_send()


def fused(n, *args):
    activations, output_grads, basis_in, basis_out, query_left, query_right, owners = args[:7]
    tokens, width_in = activations.shape[1:]
    width_out = output_grads.shape[2]
    queries, rank = owners.shape[0], query_left.shape[1]
    cols = queries * rank
    d_blk, f_blk = width_in // n, width_out // n
    both = d_blk + f_blk
    hops = n // CORES // 2 + 1
    dma = pltpu.SemaphoreType.DMA
    result = pl.pallas_call(
        functools.partial(fused_kernel, n),
        out_shape=jax.ShapeDtypeStruct((8, LANES), jnp.float32),
        in_specs=[pl.BlockSpec(memory_space=pl.ANY)] * 6
        + [pl.BlockSpec(memory_space=pltpu.SMEM)] * 3,
        out_specs=pl.BlockSpec(memory_space=pltpu.VMEM),
        scratch_shapes=[
            pltpu.VMEM((tokens, width_in), jnp.bfloat16),
            pltpu.VMEM((tokens, width_out), jnp.bfloat16),
            pltpu.VMEM(basis_in.shape, jnp.bfloat16),
            pltpu.VMEM(basis_out.shape, jnp.bfloat16),
            pltpu.VMEM((n, rank // 2, both), jnp.bfloat16),
            pltpu.VMEM((n, cols, both), jnp.bfloat16),
            pltpu.VMEM((n, both, cols), jnp.bfloat16),
            pltpu.VMEM((d_blk, cols), jnp.float32),
            pltpu.VMEM((f_blk, cols), jnp.float32),
            pltpu.VMEM((tokens, cols), jnp.float32),
            pltpu.VMEM((tokens, cols), jnp.float32),
            pltpu.VMEM((n, 8, LANES), jnp.float32),
            dma((7,)),
            dma((2,)),
            dma((n, 2)),
            dma((n, 2)),
            dma,
            dma,
            dma((2, 2, 2, hops)),
            dma((2, 2, 2, hops)),
            dma((2, 2, 2, hops)),
            dma((2, 2, 2, hops)),
            dma((n,)),
            dma((n,)),
        ],
        compiler_params=pltpu.CompilerParams(
            collective_id=0, has_side_effects=True, vmem_limit_bytes=60 * 1024 * 1024
        ),
    )(*args)
    return result[:1, :queries]


def spread(value, axis, source):
    kept = jnp.where(lax.axis_index(axis) == source, value, 0).astype(value.dtype)
    return lax.psum(kept, axis)


def plain(
    activations,
    output_grads,
    basis_in,
    basis_out,
    query_left,
    query_right,
    owners,
    lengths,
    slot_plan,
):
    num_blocks = lax.axis_size("blk")
    my_index = lax.axis_index("blk")
    seqs_here = activations.shape[0]
    max_length = activations.shape[1]
    num_queries = owners.shape[0]
    rank_count = query_left.shape[1]
    total_seqs = seqs_here * num_blocks
    total_cols = num_queries * rank_count
    pieces_in = [spread(query_left[0], "blk", owners[q]) for q in range(num_queries)]
    pieces_out = [spread(query_right[0], "blk", owners[q]) for q in range(num_queries)]
    picked_in = jnp.stack(pieces_in).reshape(total_cols, query_left.shape[2])
    picked_out = jnp.stack(pieces_out).reshape(total_cols, query_right.shape[2])
    contract = (((1,), (1,)), ((), ()))
    rotated_in = lax.dot_general(
        basis_in, picked_in, contract, preferred_element_type=jnp.float32
    ).astype(jnp.bfloat16)
    rotated_out = lax.dot_general(
        basis_out, picked_out, contract, preferred_element_type=jnp.float32
    ).astype(jnp.bfloat16)
    slot_match = slot_plan[:, None] == jnp.arange(total_seqs, dtype=jnp.int32)[None, :]
    slot_lengths = jnp.sum(jnp.where(slot_match, lengths[None, :], 0), axis=1)
    live_all = (jnp.arange(max_length, dtype=jnp.int32)[None, :] < slot_lengths[:, None]).astype(
        jnp.float32
    )
    my_live = lax.dynamic_slice_in_dim(live_all, my_index * seqs_here, seqs_here, 0)
    flat_in = activations.reshape(-1, activations.shape[2])
    flat_out = output_grads.reshape(-1, output_grads.shape[2])
    whole_in = lax.all_gather(rotated_in, "blk", axis=0, tiled=True)
    whole_out = lax.all_gather(rotated_out, "blk", axis=0, tiled=True)
    project_in = jnp.dot(flat_in, whole_in, preferred_element_type=jnp.float32)
    project_out = jnp.dot(flat_out, whole_out, preferred_element_type=jnp.float32)
    products = (project_in * project_out).reshape(-1, max_length, num_queries, rank_count)
    gathered = lax.all_gather(
        jnp.einsum("stqr,st->sq", products, my_live) / rank_count, "blk", axis=0, tiled=True
    )
    seq_ids = my_index * seqs_here + jnp.arange(seqs_here, dtype=jnp.int32)
    chooser = (slot_plan[None, :] == seq_ids[:, None]).astype(jnp.float32)
    return jnp.dot(chooser, gathered, precision=lax.Precision.HIGHEST)


def shards(*args):
    n = lax.axis_size("blk")
    activations, output_grads, basis_in, basis_out, query_left, _, owners = args[:7]
    queries, rank = owners.shape[0], query_left.shape[1]
    fits = (
        lax.axis_size("parts") == 2
        and n % (2 * CORES) == 0
        and n >= 4 * CORES
        and activations.shape[0] == 1
        and query_left.shape[0] == 1
        and activations.shape[2] % (n * LANES) == 0
        and output_grads.shape[2] % (n * LANES) == 0
        and (activations.shape[2] + output_grads.shape[2]) // n % 32 == 0
        and basis_in.shape[0] * n == activations.shape[2]
        and basis_out.shape[0] * n == output_grads.shape[2]
        and basis_out.shape[0] % 64 == 0
        and queries * rank == LANES
        and rank % 32 == 0
    )
    return fused(n, *args) if fits else plain(*args)


def solution(mesh):
    placed = (
        P(("parts", "blk"), None, None),
        P(("parts", "blk"), None, None),
        P("blk", None),
        P("blk", None),
        P("blk", None, None),
        P("blk", None, None),
        P(),
        P("parts"),
        P("parts"),
    )
    return jax.shard_map(
        shards, mesh=mesh, in_specs=placed, out_specs=P(("parts", "blk"), None), check_vma=False
    )
```

```python
import functools

import jax
import jax.numpy as jnp
from jax import lax
from jax.experimental import pallas as pl
from jax.experimental.pallas import tpu as pltpu
from jax.sharding import PartitionSpec as P

MESH = pl.DeviceIdType.MESH
CORES = 2
LANES = 128


def ring_order(chips):
    cols = 1
    while (2 * cols) * (2 * cols) <= chips:
        cols *= 2
    rows = chips // cols
    tour = [r * cols for r in range(rows)]
    for step, r in enumerate(reversed(range(rows))):
        across = range(1, cols) if step % 2 == 0 else range(cols - 1, 0, -1)
        tour += [r * cols + c for c in across]
    return tour


def lookup(index, table):
    found = jnp.int32(0)
    for key, value in enumerate(table):
        found = found + jnp.where(index == key, jnp.int32(value), jnp.int32(0))
    return found


def fused_kernel(
    n,
    act_hbm,
    grad_hbm,
    bin_hbm,
    bout_hbm,
    ql_hbm,
    qr_hbm,
    owners,
    lengths,
    slot_plan,
    out_ref,
    act,
    grad,
    bin_,
    bout,
    slots,
    gathered,
    rotated,
    acc_in,
    acc_out,
    proj_in,
    proj_out,
    tiles,
    load_sem,
    own_sem,
    a2a_send,
    a2a_recv,
    trade_send,
    trade_recv,
    x_send,
    x_recv,
    ring_send,
    ring_recv,
    sib_send,
    sib_recv,
    tile_send,
    tile_recv,
):
    part = lax.axis_index("parts")
    me = lax.axis_index("blk")
    chips = n // CORES
    core = lax.rem(me, CORES)
    chip = me // CORES
    tour = ring_order(chips)
    place = lookup(chip, [tour.index(c) for c in range(chips)])
    sibling = chip * CORES + (1 - core)
    d_blk = act.shape[1] // n
    f_blk = grad.shape[1] // n
    both = d_blk + f_blk
    rank = ql_hbm.shape[1]
    half_rank = rank // 2
    queries = owners.shape[0]
    sub_rows = queries * half_rank
    far = chips // 2

    def at_distance(h, way, which_core):
        spot = lax.rem(place - h + chips, chips) if way == 0 else lax.rem(place + h, chips)
        return lookup(spot, tour) * CORES + which_core

    right = at_distance(1, 1, core)
    left = at_distance(1, 0, core)

    loads = []

    def load(src, dst):
        copy = pltpu.make_async_copy(src, dst, load_sem.at[len(loads)])
        copy.start()
        loads.append(copy)

    barrier = pltpu.get_barrier_semaphore()
    for k in range(1, n):
        pl.semaphore_signal(
            barrier, inc=1, device_id={"blk": lax.rem(me + k, n)}, device_id_type=MESH
        )
    pl.semaphore_signal(barrier, inc=1, device_id={"parts": 1 - part}, device_id_type=MESH)

    my_rows = pl.ds(pl.multiple_of(part * half_rank, half_rank), half_rank)

    def cut(target, width):
        return pl.ds(pl.multiple_of(target * width, LANES), width)

    own = [
        pltpu.make_async_copy(
            ql_hbm.at[0, my_rows, cut(me, d_blk)], slots.at[me, :, pl.ds(0, d_blk)], own_sem.at[0]
        ),
        pltpu.make_async_copy(
            qr_hbm.at[0, my_rows, cut(me, f_blk)],
            slots.at[me, :, pl.ds(d_blk, f_blk)],
            own_sem.at[1],
        ),
    ]
    for copy in own:
        copy.start()
    pl.semaphore_wait(barrier, n)

    swaps = []
    for k in range(1, n):
        target = lax.rem(me + k, n)
        for piece, (src, width, start) in enumerate(((ql_hbm, d_blk, 0), (qr_hbm, f_blk, d_blk))):
            copy = pltpu.make_async_remote_copy(
                src_ref=src.at[0, my_rows, cut(target, width)],
                dst_ref=slots.at[me, :, pl.ds(start, width)],
                send_sem=a2a_send.at[k, piece],
                recv_sem=a2a_recv.at[k, piece],
                device_id={"blk": target},
                device_id_type=MESH,
            )
            copy.start()
            swaps.append(copy)

    load(bin_hbm, bin_)
    quarter = bout.shape[0] // 4
    for i in range(4):
        span = pl.ds(i * quarter, quarter)
        load(bout_hbm.at[span], bout.at[span])
    load(act_hbm.at[0], act)
    load(grad_hbm.at[0], grad)
    acc_in[...] = jnp.zeros_like(acc_in)
    acc_out[...] = jnp.zeros_like(acc_out)
    proj_in[...] = jnp.zeros_like(proj_in)
    proj_out[...] = jnp.zeros_like(proj_out)

    for copy in own:
        copy.wait()
    for copy in swaps:
        copy.wait_recv()
    first = pl.multiple_of(part * sub_rows, sub_rows)
    for q in range(queries):
        gathered[me, pl.ds(pl.multiple_of(first + q * half_rank, half_rank), half_rank), :] = slots[
            owners[q]
        ]

    def spread(buffer, phase, subs, crossing, whole, before_sub, compute):
        limit = ((far, far - 1), (far, far - 1), (far - 1, far))
        started = []

        def remote(view, send_sem, recv_sem, device):
            return pltpu.make_async_remote_copy(
                src_ref=view,
                dst_ref=view,
                send_sem=send_sem,
                recv_sem=recv_sem,
                device_id=device,
                device_id_type=MESH,
            )

        def ring(u, way, h, at):
            return remote(
                buffer.at[at_distance(at, way, core), subs[u]],
                ring_send.at[phase, u, way, h],
                ring_recv.at[phase, u, way, h],
                {"blk": right if way == 0 else left},
            )

        def across(way, h, rows):
            return remote(
                buffer.at[at_distance(h, way, core), rows],
                x_send.at[phase, way, h],
                x_recv.at[phase, way, h],
                {"parts": 1 - part},
            )

        def aside(u, way, h, which_core):
            return remote(
                buffer.at[at_distance(h, way, which_core), subs[u] if u < 3 else crossing],
                sib_send.at[phase, u, way, h],
                sib_recv.at[phase, u, way, h],
                {"blk": sibling},
            )

        def go(copy):
            copy.start()
            started.append(copy)

        def ways_of(u, h):
            return [w for w in range(2) if h <= limit[u][w]] if h else [0]

        def finish_own(h):
            for way in ways_of(0, h):
                if h or not whole:
                    across(way, h, crossing).wait_recv()
                go(aside(3, way, h, core))
            directions = [0] if h in (0, far) else [0, 1]
            compute([at_distance(h, way, core) for way in directions], h == 0)

        def finish_other(h):
            for u in range(4):
                for way in ways_of(u % 3, h):
                    aside(u, way, h, 1 - core).wait_recv()
            directions = [0] if h in (0, far) else [0, 1]
            compute([at_distance(h, way, 1 - core) for way in directions], False)

        for h in range(far + 1):
            for u in range(3):
                if h == 0:
                    before_sub(u)
                for way in ways_of(u, h):
                    if h:
                        ring(u, way, h - 1, h).wait_recv()
                        if h < limit[u][way]:
                            go(ring(u, way, h, h))
                    else:
                        go(ring(u, 0, 0, 0))
                        go(ring(u, 1, 0, 0))
                    if u == 0 and (h or not whole):
                        go(across(way, h, subs[0]))
                    go(aside(u, way, h, core))
                if h and u == 0:
                    finish_own(h - 1)
                if h and u == 1:
                    finish_other(h - 1)
        finish_own(far)
        finish_other(far)
        return started

    over_last = (((1,), (1,)), ((), ()))

    def each(blocks, body):
        def step(i, carry):
            block = blocks[0]
            for k in range(1, len(blocks)):
                block = jnp.where(i == k, blocks[k], block)
            body(block)
            return carry

        lax.fori_loop(0, len(blocks), step, 0)

    def rotate(block):
        acc_in[...] += lax.dot_general(
            bin_[:, cut(block, d_blk)],
            gathered[block, :, 0:d_blk],
            over_last,
            preferred_element_type=jnp.float32,
        )
        acc_out[...] += lax.dot_general(
            bout[:, cut(block, f_blk)],
            gathered[block, :, d_blk:both],
            over_last,
            preferred_element_type=jnp.float32,
        )

    def rotate_all(blocks, opening):
        if opening:
            for copy in loads:
                copy.wait()
        each(blocks, rotate)

    def layout(unit):
        def span(start, count):
            return pl.ds(pl.multiple_of(start * unit, unit), count * unit)

        subs = [span(part * 6, 2), span(2 + part * 3, 1), span(3 - part, 3)]
        return subs, span(6 - part * 6, 2), span

    query_subs, query_crossing, query_span = layout(gathered.shape[1] // 8)

    def trade(start):
        rows = query_span(start, 2)
        return pltpu.make_async_remote_copy(
            src_ref=gathered.at[me, rows],
            dst_ref=gathered.at[me, rows],
            send_sem=trade_send,
            recv_sem=trade_recv,
            device_id={"parts": 1 - part},
            device_id_type=MESH,
        )

    traded = trade(2 + 2 * part)
    traded.start()

    def before_rotate(u):
        if u == 2:
            trade(4 - 2 * part).wait_recv()

    started = spread(gathered, 0, query_subs, query_crossing, False, before_rotate, rotate_all)

    rotated[me, 0:d_blk, :] = acc_in[...].astype(rotated.dtype)
    rotated[me, d_blk:both, :] = acc_out[...].astype(rotated.dtype)

    def project(block):
        proj_in[...] += jnp.dot(
            act[:, cut(block, d_blk)],
            rotated[block, 0:d_blk, :],
            preferred_element_type=jnp.float32,
        )
        proj_out[...] += jnp.dot(
            grad[:, cut(block, f_blk)],
            rotated[block, d_blk:both, :],
            preferred_element_type=jnp.float32,
        )

    block_subs, block_crossing, _ = layout(both // 8)
    started += spread(
        rotated,
        1,
        block_subs,
        block_crossing,
        True,
        lambda u: None,
        lambda blocks, opening: each(blocks, project),
    )

    length = lengths[slot_plan[me]]
    times = lax.broadcasted_iota(jnp.int32, proj_in.shape, 0)
    product = jnp.where(times < length, proj_in[...] * proj_out[...], 0.0)
    by_col = jnp.sum(product, axis=0, keepdims=True)
    col = lax.broadcasted_iota(jnp.int32, by_col.shape, 1)
    col_query = lax.rem(col // half_rank, queries)
    score = jnp.zeros((8, LANES), jnp.float32)
    lane = lax.broadcasted_iota(jnp.int32, score.shape, 1)
    for q in range(queries):
        total = jnp.sum(jnp.where(col_query == q, by_col, 0.0), axis=1, keepdims=True) / rank
        score = jnp.where(lane == q, total, score)
    tiles[me] = score
    pushes = []
    for k in range(1, n):
        copy = pltpu.make_async_remote_copy(
            src_ref=tiles.at[me],
            dst_ref=tiles.at[me],
            send_sem=tile_send.at[k],
            recv_sem=tile_recv.at[k],
            device_id={"blk": lax.rem(me + k, n)},
            device_id_type=MESH,
        )
        copy.start()
        pushes.append(copy)
    for k in range(1, n):
        source = lax.rem(me - k + n, n)
        pltpu.make_async_remote_copy(
            src_ref=tiles.at[source],
            dst_ref=tiles.at[source],
            send_sem=tile_send.at[k],
            recv_sem=tile_recv.at[k],
            device_id={"blk": lax.rem(me + k, n)},
            device_id_type=MESH,
        ).wait_recv()
    mine = jnp.zeros((8, LANES), jnp.float32)
    for j in range(n):
        mine = jnp.where(slot_plan[j] == me, tiles[j], mine)
    out_ref[...] = mine
    for copy in swaps + [traded] + started + pushes:
        copy.wait_send()


def fused(n, *args):
    activations, output_grads, basis_in, basis_out, query_left, query_right, owners = args[:7]
    tokens, width_in = activations.shape[1:]
    width_out = output_grads.shape[2]
    queries, rank = owners.shape[0], query_left.shape[1]
    cols = queries * rank
    d_blk, f_blk = width_in // n, width_out // n
    both = d_blk + f_blk
    hops = n // CORES // 2 + 1
    dma = pltpu.SemaphoreType.DMA
    result = pl.pallas_call(
        functools.partial(fused_kernel, n),
        out_shape=jax.ShapeDtypeStruct((8, LANES), jnp.float32),
        in_specs=[pl.BlockSpec(memory_space=pl.ANY)] * 6
        + [pl.BlockSpec(memory_space=pltpu.SMEM)] * 3,
        out_specs=pl.BlockSpec(memory_space=pltpu.VMEM),
        scratch_shapes=[
            pltpu.VMEM((tokens, width_in), jnp.bfloat16),
            pltpu.VMEM((tokens, width_out), jnp.bfloat16),
            pltpu.VMEM(basis_in.shape, jnp.bfloat16),
            pltpu.VMEM(basis_out.shape, jnp.bfloat16),
            pltpu.VMEM((n, rank // 2, both), jnp.bfloat16),
            pltpu.VMEM((n, cols, both), jnp.bfloat16),
            pltpu.VMEM((n, both, cols), jnp.bfloat16),
            pltpu.VMEM((d_blk, cols), jnp.float32),
            pltpu.VMEM((f_blk, cols), jnp.float32),
            pltpu.VMEM((tokens, cols), jnp.float32),
            pltpu.VMEM((tokens, cols), jnp.float32),
            pltpu.VMEM((n, 8, LANES), jnp.float32),
            dma((7,)),
            dma((2,)),
            dma((n, 2)),
            dma((n, 2)),
            dma,
            dma,
            dma((2, 2, hops)),
            dma((2, 2, hops)),
            dma((2, 3, 2, hops)),
            dma((2, 3, 2, hops)),
            dma((2, 4, 2, hops)),
            dma((2, 4, 2, hops)),
            dma((n,)),
            dma((n,)),
        ],
        compiler_params=pltpu.CompilerParams(
            collective_id=0, has_side_effects=True, vmem_limit_bytes=60 * 1024 * 1024
        ),
    )(*args)
    return result[:1, :queries]


def spread(value, axis, source):
    kept = jnp.where(lax.axis_index(axis) == source, value, 0).astype(value.dtype)
    return lax.psum(kept, axis)


def plain(
    activations,
    output_grads,
    basis_in,
    basis_out,
    query_left,
    query_right,
    owners,
    lengths,
    slot_plan,
):
    num_blocks = lax.axis_size("blk")
    my_index = lax.axis_index("blk")
    seqs_here = activations.shape[0]
    max_length = activations.shape[1]
    num_queries = owners.shape[0]
    rank_count = query_left.shape[1]
    total_seqs = seqs_here * num_blocks
    total_cols = num_queries * rank_count
    pieces_in = [spread(query_left[0], "blk", owners[q]) for q in range(num_queries)]
    pieces_out = [spread(query_right[0], "blk", owners[q]) for q in range(num_queries)]
    picked_in = jnp.stack(pieces_in).reshape(total_cols, query_left.shape[2])
    picked_out = jnp.stack(pieces_out).reshape(total_cols, query_right.shape[2])
    contract = (((1,), (1,)), ((), ()))
    rotated_in = lax.dot_general(
        basis_in, picked_in, contract, preferred_element_type=jnp.float32
    ).astype(jnp.bfloat16)
    rotated_out = lax.dot_general(
        basis_out, picked_out, contract, preferred_element_type=jnp.float32
    ).astype(jnp.bfloat16)
    slot_match = slot_plan[:, None] == jnp.arange(total_seqs, dtype=jnp.int32)[None, :]
    slot_lengths = jnp.sum(jnp.where(slot_match, lengths[None, :], 0), axis=1)
    live_all = (jnp.arange(max_length, dtype=jnp.int32)[None, :] < slot_lengths[:, None]).astype(
        jnp.float32
    )
    my_live = lax.dynamic_slice_in_dim(live_all, my_index * seqs_here, seqs_here, 0)
    flat_in = activations.reshape(-1, activations.shape[2])
    flat_out = output_grads.reshape(-1, output_grads.shape[2])
    whole_in = lax.all_gather(rotated_in, "blk", axis=0, tiled=True)
    whole_out = lax.all_gather(rotated_out, "blk", axis=0, tiled=True)
    project_in = jnp.dot(flat_in, whole_in, preferred_element_type=jnp.float32)
    project_out = jnp.dot(flat_out, whole_out, preferred_element_type=jnp.float32)
    products = (project_in * project_out).reshape(-1, max_length, num_queries, rank_count)
    gathered = lax.all_gather(
        jnp.einsum("stqr,st->sq", products, my_live) / rank_count, "blk", axis=0, tiled=True
    )
    seq_ids = my_index * seqs_here + jnp.arange(seqs_here, dtype=jnp.int32)
    chooser = (slot_plan[None, :] == seq_ids[:, None]).astype(jnp.float32)
    return jnp.dot(chooser, gathered, precision=lax.Precision.HIGHEST)


def shards(*args):
    n = lax.axis_size("blk")
    activations, output_grads, basis_in, basis_out, query_left, _, owners = args[:7]
    queries, rank = owners.shape[0], query_left.shape[1]
    fits = (
        lax.axis_size("parts") == 2
        and n % (2 * CORES) == 0
        and n >= 4 * CORES
        and activations.shape[0] == 1
        and query_left.shape[0] == 1
        and activations.shape[2] % (n * LANES) == 0
        and output_grads.shape[2] % (n * LANES) == 0
        and (activations.shape[2] + output_grads.shape[2]) // n % 128 == 0
        and basis_in.shape[0] * n == activations.shape[2]
        and basis_out.shape[0] * n == output_grads.shape[2]
        and basis_out.shape[0] % 64 == 0
        and queries * rank == LANES
        and rank % 32 == 0
    )
    return fused(n, *args) if fits else plain(*args)


def solution(mesh):
    placed = (
        P(("parts", "blk"), None, None),
        P(("parts", "blk"), None, None),
        P("blk", None),
        P("blk", None),
        P("blk", None, None),
        P("blk", None, None),
        P(),
        P("parts"),
        P("parts"),
    )
    return jax.shard_map(
        shards, mesh=mesh, in_specs=placed, out_specs=P(("parts", "blk"), None), check_vma=False
    )
```

```python
import functools

import jax
import jax.numpy as jnp
from jax import lax
from jax.experimental import pallas as pl
from jax.experimental.pallas import tpu as pltpu
from jax.sharding import PartitionSpec as P

MESH = pl.DeviceIdType.MESH
CORES = 2
LANES = 128


def ring_order(chips):
    cols = 1
    while (2 * cols) * (2 * cols) <= chips:
        cols *= 2
    rows = chips // cols
    tour = [r * cols for r in range(rows)]
    for step, r in enumerate(reversed(range(rows))):
        across = range(1, cols) if step % 2 == 0 else range(cols - 1, 0, -1)
        tour += [r * cols + c for c in across]
    return tour


def lookup(index, table):
    found = jnp.int32(0)
    for key, value in enumerate(table):
        found = found + jnp.where(index == key, jnp.int32(value), jnp.int32(0))
    return found


def fused_kernel(
    n,
    act_hbm,
    grad_hbm,
    bin_hbm,
    bout_hbm,
    ql_hbm,
    qr_hbm,
    owners,
    lengths,
    slot_plan,
    out_ref,
    act,
    grad,
    bin_,
    bout,
    slots,
    gathered,
    rotated,
    acc_in,
    acc_out,
    proj_in,
    proj_out,
    tiles,
    load_sem,
    own_sem,
    a2a_send,
    a2a_recv,
    trade_send,
    trade_recv,
    x_send,
    x_recv,
    ring_send,
    ring_recv,
    sib_send,
    sib_recv,
    tile_send,
    tile_recv,
):
    part = lax.axis_index("parts")
    me = lax.axis_index("blk")
    chips = n // CORES
    core = lax.rem(me, CORES)
    chip = me // CORES
    tour = ring_order(chips)
    place = lookup(chip, [tour.index(c) for c in range(chips)])
    sibling = chip * CORES + (1 - core)
    d_blk = act.shape[1] // n
    f_blk = grad.shape[1] // n
    both = d_blk + f_blk
    rank = ql_hbm.shape[1]
    half_rank = rank // 2
    queries = owners.shape[0]
    sub_rows = queries * half_rank
    far = chips // 2

    def at_distance(h, way, which_core):
        spot = lax.rem(place - h + chips, chips) if way == 0 else lax.rem(place + h, chips)
        return lookup(spot, tour) * CORES + which_core

    right = at_distance(1, 1, core)
    left = at_distance(1, 0, core)

    loads = []

    def load(src, dst):
        copy = pltpu.make_async_copy(src, dst, load_sem.at[len(loads)])
        copy.start()
        loads.append(copy)

    barrier = pltpu.get_barrier_semaphore()
    for k in range(1, n):
        pl.semaphore_signal(
            barrier, inc=1, device_id={"blk": lax.rem(me + k, n)}, device_id_type=MESH
        )
    pl.semaphore_signal(barrier, inc=1, device_id={"parts": 1 - part}, device_id_type=MESH)

    my_rows = pl.ds(pl.multiple_of(part * half_rank, half_rank), half_rank)

    def cut(target, width):
        return pl.ds(pl.multiple_of(target * width, LANES), width)

    own = [
        pltpu.make_async_copy(
            ql_hbm.at[0, my_rows, cut(me, d_blk)], slots.at[me, :, pl.ds(0, d_blk)], own_sem.at[0]
        ),
        pltpu.make_async_copy(
            qr_hbm.at[0, my_rows, cut(me, f_blk)],
            slots.at[me, :, pl.ds(d_blk, f_blk)],
            own_sem.at[1],
        ),
    ]
    for copy in own:
        copy.start()
    load(bin_hbm, bin_)
    quarter = bout.shape[0] // 4
    for i in range(4):
        span = pl.ds(i * quarter, quarter)
        load(bout_hbm.at[span], bout.at[span])
    load(act_hbm.at[0], act)
    load(grad_hbm.at[0], grad)
    pl.semaphore_wait(barrier, n)

    swaps = []
    for k in range(1, n):
        target = lax.rem(me + k, n)
        for piece, (src, width, start) in enumerate(((ql_hbm, d_blk, 0), (qr_hbm, f_blk, d_blk))):
            copy = pltpu.make_async_remote_copy(
                src_ref=src.at[0, my_rows, cut(target, width)],
                dst_ref=slots.at[me, :, pl.ds(start, width)],
                send_sem=a2a_send.at[k, piece],
                recv_sem=a2a_recv.at[k, piece],
                device_id={"blk": target},
                device_id_type=MESH,
            )
            copy.start()
            swaps.append(copy)

    acc_in[...] = jnp.zeros_like(acc_in)
    acc_out[...] = jnp.zeros_like(acc_out)
    proj_in[...] = jnp.zeros_like(proj_in)
    proj_out[...] = jnp.zeros_like(proj_out)

    for copy in own:
        copy.wait()
    for copy in swaps:
        copy.wait_recv()
    first = pl.multiple_of(part * sub_rows, sub_rows)
    for q in range(queries):
        gathered[me, pl.ds(pl.multiple_of(first + q * half_rank, half_rank), half_rank), :] = slots[
            owners[q]
        ]

    def spread(buffer, phase, subs, crossing, whole, before_sub, compute):
        limit = ((far, far - 1), (far, far - 1), (far - 1, far))
        started = []

        def remote(view, send_sem, recv_sem, device):
            return pltpu.make_async_remote_copy(
                src_ref=view,
                dst_ref=view,
                send_sem=send_sem,
                recv_sem=recv_sem,
                device_id=device,
                device_id_type=MESH,
            )

        def ring(u, way, h, at):
            return remote(
                buffer.at[at_distance(at, way, core), subs[u]],
                ring_send.at[phase, u, way, h],
                ring_recv.at[phase, u, way, h],
                {"blk": right if way == 0 else left},
            )

        def across(way, h, rows):
            return remote(
                buffer.at[at_distance(h, way, core), rows],
                x_send.at[phase, way, h],
                x_recv.at[phase, way, h],
                {"parts": 1 - part},
            )

        def aside(u, way, h, which_core):
            return remote(
                buffer.at[at_distance(h, way, which_core), subs[u] if u < 3 else crossing],
                sib_send.at[phase, u, way, h],
                sib_recv.at[phase, u, way, h],
                {"blk": sibling},
            )

        def go(copy):
            copy.start()
            started.append(copy)

        def ways_of(u, h):
            return [w for w in range(2) if h <= limit[u][w]] if h else [0]

        def finish_own(h):
            def crossed():
                for way in ways_of(0, h):
                    if h or not whole:
                        across(way, h, crossing).wait_recv()
                    go(aside(3, way, h, core))

            return [crossed] + [
                functools.partial(compute, [at_distance(h, way, core)], h == 0)
                for way in both_ways(h)
            ]

        def finish_other(h):
            def arrived():
                for u in range(4):
                    for way in ways_of(u % 3, h):
                        aside(u, way, h, 1 - core).wait_recv()

            return [arrived] + [
                functools.partial(compute, [at_distance(h, way, 1 - core)], False)
                for way in both_ways(h)
            ]

        def both_ways(h):
            return [0] if h in (0, far) else [0, 1]

        for h in range(far + 1):
            for u in range(3):
                if h == 0:
                    before_sub(u)
                for way in ways_of(u, h):
                    if h:
                        ring(u, way, h - 1, h).wait_recv()
                        if h < limit[u][way]:
                            go(ring(u, way, h, h))
                    else:
                        go(ring(u, 0, 0, 0))
                        go(ring(u, 1, 0, 0))
                    if u == 0 and (h or not whole):
                        go(across(way, h, subs[0]))
                    go(aside(u, way, h, core))
                if h:
                    if u == 0:
                        tasks = finish_own(h - 1) + finish_other(h - 1)
                    for _ in range((2, 4, len(tasks))[u]):
                        if tasks:
                            tasks.pop(0)()
        for task in finish_own(far) + finish_other(far):
            task()
        return started

    over_last = (((1,), (1,)), ((), ()))

    def each(blocks, body):
        def step(i, carry):
            block = blocks[0]
            for k in range(1, len(blocks)):
                block = jnp.where(i == k, blocks[k], block)
            body(block)
            return carry

        lax.fori_loop(0, len(blocks), step, 0)

    def rotate(block):
        acc_in[...] += lax.dot_general(
            bin_[:, cut(block, d_blk)],
            gathered[block, :, 0:d_blk],
            over_last,
            preferred_element_type=jnp.float32,
        )
        acc_out[...] += lax.dot_general(
            bout[:, cut(block, f_blk)],
            gathered[block, :, d_blk:both],
            over_last,
            preferred_element_type=jnp.float32,
        )

    def rotate_all(blocks, opening):
        if opening:
            for copy in loads:
                copy.wait()
        each(blocks, rotate)

    def layout(unit):
        def span(start, count):
            return pl.ds(pl.multiple_of(start * unit, unit), count * unit)

        subs = [span(part * 6, 2), span(2 + part * 3, 1), span(3 - part, 3)]
        return subs, span(6 - part * 6, 2), span

    query_subs, query_crossing, query_span = layout(gathered.shape[1] // 8)

    def trade(start):
        rows = query_span(start, 2)
        return pltpu.make_async_remote_copy(
            src_ref=gathered.at[me, rows],
            dst_ref=gathered.at[me, rows],
            send_sem=trade_send,
            recv_sem=trade_recv,
            device_id={"parts": 1 - part},
            device_id_type=MESH,
        )

    traded = trade(2 + 2 * part)
    traded.start()

    def before_rotate(u):
        if u == 2:
            trade(4 - 2 * part).wait_recv()

    started = spread(gathered, 0, query_subs, query_crossing, False, before_rotate, rotate_all)

    rotated[me, 0:d_blk, :] = acc_in[...].astype(rotated.dtype)
    rotated[me, d_blk:both, :] = acc_out[...].astype(rotated.dtype)

    def project(block):
        proj_in[...] += jnp.dot(
            act[:, cut(block, d_blk)],
            rotated[block, 0:d_blk, :],
            preferred_element_type=jnp.float32,
        )
        proj_out[...] += jnp.dot(
            grad[:, cut(block, f_blk)],
            rotated[block, d_blk:both, :],
            preferred_element_type=jnp.float32,
        )

    cross = both * 5 // 18 // 16 * 16
    light = (both - 3 * cross) // 32 * 16

    def rows(if_first, if_second, count):
        return pl.ds(pl.multiple_of(if_first + part * (if_second - if_first), 16), count)

    block_subs = [
        rows(0, both - cross, cross),
        rows(cross, both - cross - light, light),
        rows(cross + light, cross, both - 2 * cross - light),
    ]
    block_crossing = rows(both - cross, 0, cross)
    started += spread(
        rotated,
        1,
        block_subs,
        block_crossing,
        True,
        lambda u: None,
        lambda blocks, opening: each(blocks, project),
    )

    length = lengths[slot_plan[me]]
    times = lax.broadcasted_iota(jnp.int32, proj_in.shape, 0)
    product = jnp.where(times < length, proj_in[...] * proj_out[...], 0.0)
    by_col = jnp.sum(product, axis=0, keepdims=True)
    col = lax.broadcasted_iota(jnp.int32, by_col.shape, 1)
    col_query = lax.rem(col // half_rank, queries)
    score = jnp.zeros((8, LANES), jnp.float32)
    lane = lax.broadcasted_iota(jnp.int32, score.shape, 1)
    for q in range(queries):
        total = jnp.sum(jnp.where(col_query == q, by_col, 0.0), axis=1, keepdims=True) / rank
        score = jnp.where(lane == q, total, score)
    tiles[me] = score
    pushes = []
    for k in range(1, n):
        copy = pltpu.make_async_remote_copy(
            src_ref=tiles.at[me],
            dst_ref=tiles.at[me],
            send_sem=tile_send.at[k],
            recv_sem=tile_recv.at[k],
            device_id={"blk": lax.rem(me + k, n)},
            device_id_type=MESH,
        )
        copy.start()
        pushes.append(copy)
    for k in range(1, n):
        source = lax.rem(me - k + n, n)
        pltpu.make_async_remote_copy(
            src_ref=tiles.at[source],
            dst_ref=tiles.at[source],
            send_sem=tile_send.at[k],
            recv_sem=tile_recv.at[k],
            device_id={"blk": lax.rem(me + k, n)},
            device_id_type=MESH,
        ).wait_recv()
    mine = jnp.zeros((8, LANES), jnp.float32)
    for j in range(n):
        mine = jnp.where(slot_plan[j] == me, tiles[j], mine)
    out_ref[...] = mine[:1, :queries]
    for copy in swaps + [traded] + started + pushes:
        copy.wait_send()


def fused(n, *args):
    activations, output_grads, basis_in, basis_out, query_left, query_right, owners = args[:7]
    tokens, width_in = activations.shape[1:]
    width_out = output_grads.shape[2]
    queries, rank = owners.shape[0], query_left.shape[1]
    cols = queries * rank
    d_blk, f_blk = width_in // n, width_out // n
    both = d_blk + f_blk
    hops = n // CORES // 2 + 1
    dma = pltpu.SemaphoreType.DMA
    return pl.pallas_call(
        functools.partial(fused_kernel, n),
        out_shape=jax.ShapeDtypeStruct((1, queries), jnp.float32),
        in_specs=[pl.BlockSpec(memory_space=pl.ANY)] * 6
        + [pl.BlockSpec(memory_space=pltpu.SMEM)] * 3,
        out_specs=pl.BlockSpec(memory_space=pltpu.VMEM),
        scratch_shapes=[
            pltpu.VMEM((tokens, width_in), jnp.bfloat16),
            pltpu.VMEM((tokens, width_out), jnp.bfloat16),
            pltpu.VMEM(basis_in.shape, jnp.bfloat16),
            pltpu.VMEM(basis_out.shape, jnp.bfloat16),
            pltpu.VMEM((n, rank // 2, both), jnp.bfloat16),
            pltpu.VMEM((n, cols, both), jnp.bfloat16),
            pltpu.VMEM((n, both, cols), jnp.bfloat16),
            pltpu.VMEM((d_blk, cols), jnp.float32),
            pltpu.VMEM((f_blk, cols), jnp.float32),
            pltpu.VMEM((tokens, cols), jnp.float32),
            pltpu.VMEM((tokens, cols), jnp.float32),
            pltpu.VMEM((n, 8, LANES), jnp.float32),
            dma((7,)),
            dma((2,)),
            dma((n, 2)),
            dma((n, 2)),
            dma,
            dma,
            dma((2, 2, hops)),
            dma((2, 2, hops)),
            dma((2, 3, 2, hops)),
            dma((2, 3, 2, hops)),
            dma((2, 4, 2, hops)),
            dma((2, 4, 2, hops)),
            dma((n,)),
            dma((n,)),
        ],
        compiler_params=pltpu.CompilerParams(
            collective_id=0, has_side_effects=True, vmem_limit_bytes=60 * 1024 * 1024
        ),
    )(*args)


def spread(value, axis, source):
    kept = jnp.where(lax.axis_index(axis) == source, value, 0).astype(value.dtype)
    return lax.psum(kept, axis)


def plain(
    activations,
    output_grads,
    basis_in,
    basis_out,
    query_left,
    query_right,
    owners,
    lengths,
    slot_plan,
):
    num_blocks = lax.axis_size("blk")
    my_index = lax.axis_index("blk")
    seqs_here = activations.shape[0]
    max_length = activations.shape[1]
    num_queries = owners.shape[0]
    rank_count = query_left.shape[1]
    total_seqs = seqs_here * num_blocks
    total_cols = num_queries * rank_count
    pieces_in = [spread(query_left[0], "blk", owners[q]) for q in range(num_queries)]
    pieces_out = [spread(query_right[0], "blk", owners[q]) for q in range(num_queries)]
    picked_in = jnp.stack(pieces_in).reshape(total_cols, query_left.shape[2])
    picked_out = jnp.stack(pieces_out).reshape(total_cols, query_right.shape[2])
    contract = (((1,), (1,)), ((), ()))
    rotated_in = lax.dot_general(
        basis_in, picked_in, contract, preferred_element_type=jnp.float32
    ).astype(jnp.bfloat16)
    rotated_out = lax.dot_general(
        basis_out, picked_out, contract, preferred_element_type=jnp.float32
    ).astype(jnp.bfloat16)
    slot_match = slot_plan[:, None] == jnp.arange(total_seqs, dtype=jnp.int32)[None, :]
    slot_lengths = jnp.sum(jnp.where(slot_match, lengths[None, :], 0), axis=1)
    live_all = (jnp.arange(max_length, dtype=jnp.int32)[None, :] < slot_lengths[:, None]).astype(
        jnp.float32
    )
    my_live = lax.dynamic_slice_in_dim(live_all, my_index * seqs_here, seqs_here, 0)
    flat_in = activations.reshape(-1, activations.shape[2])
    flat_out = output_grads.reshape(-1, output_grads.shape[2])
    whole_in = lax.all_gather(rotated_in, "blk", axis=0, tiled=True)
    whole_out = lax.all_gather(rotated_out, "blk", axis=0, tiled=True)
    project_in = jnp.dot(flat_in, whole_in, preferred_element_type=jnp.float32)
    project_out = jnp.dot(flat_out, whole_out, preferred_element_type=jnp.float32)
    products = (project_in * project_out).reshape(-1, max_length, num_queries, rank_count)
    gathered = lax.all_gather(
        jnp.einsum("stqr,st->sq", products, my_live) / rank_count, "blk", axis=0, tiled=True
    )
    seq_ids = my_index * seqs_here + jnp.arange(seqs_here, dtype=jnp.int32)
    chooser = (slot_plan[None, :] == seq_ids[:, None]).astype(jnp.float32)
    return jnp.dot(chooser, gathered, precision=lax.Precision.HIGHEST)


def shards(*args):
    n = lax.axis_size("blk")
    activations, output_grads, basis_in, basis_out, query_left, _, owners = args[:7]
    queries, rank = owners.shape[0], query_left.shape[1]
    fits = (
        lax.axis_size("parts") == 2
        and n % (2 * CORES) == 0
        and n >= 4 * CORES
        and activations.shape[0] == 1
        and query_left.shape[0] == 1
        and activations.shape[2] % (n * LANES) == 0
        and output_grads.shape[2] % (n * LANES) == 0
        and (activations.shape[2] + output_grads.shape[2]) // n % 128 == 0
        and basis_in.shape[0] * n == activations.shape[2]
        and basis_out.shape[0] * n == output_grads.shape[2]
        and basis_out.shape[0] % 64 == 0
        and queries * rank == LANES
        and rank % 32 == 0
    )
    return fused(n, *args) if fits else plain(*args)


def solution(mesh):
    placed = (
        P(("parts", "blk"), None, None),
        P(("parts", "blk"), None, None),
        P("blk", None),
        P("blk", None),
        P("blk", None, None),
        P("blk", None, None),
        P(),
        P("parts"),
        P("parts"),
    )
    return jax.shard_map(
        shards, mesh=mesh, in_specs=placed, out_specs=P(("parts", "blk"), None), check_vma=False
    )
```
